32 devices in a mesh: depth: 16 (over z, y, x), samp: 2 (over core).
Axes of the slice: x: 2, y: 2, z: 4, core: 2. Of those that a mesh axis runs over, the one named last changes fastest.
Arguments:
- activations: bfloat16 [2, 16, 64, 16, 128], P('samp', 'depth'), may hold values from -6 to 6
- preact: bfloat16 [2, 16, 64, 16, 128], P('samp', 'depth'), may hold values from -6 to 6
- out_grad: bfloat16 [2, 16, 64, 16, 128], P('samp', 'depth'), may hold values from -6 to 6
- weights: bfloat16 [3, 3, 3, 128, 128], replicated, may hold values from -0.109375 to 0.109375
- master: float32 [442368], P(('depth', 'samp')), may hold values from -0.109375 to 0.109375
- moment: float32 [442368], P(('depth', 'samp')), may hold values from -4 to 4
- second: float32 [442368], P(('depth', 'samp')), may hold values from 0.1 to 1
Outputs:
- grad_input: bfloat16 [2, 16, 64, 16, 128], P('samp', 'depth')
- filter_grad: float32 [442368], P(('depth', 'samp'))
- new_moment: float32 [442368], P(('depth', 'samp'))
- new_second: float32 [442368], P(('depth', 'samp'))
- new_master: float32 [442368], P(('depth', 'samp'))
- new_weights: bfloat16 [3, 3, 3, 128, 128], replicated
The draws below stay inside these ranges and needn't reach their ends.
All inputs are finite; a program needn't handle non-finite values.
Results may differ from the reference program's by a relative error of at most 0.001.
Values may be sent and summed in bfloat16 or wider, within the bound.
No kernel may reach another device: no remote copies, remote signals or barrier semaphores. Data moves between devices by JAX's collectives and lax.ppermute only.
A program may use at most 64 MiB of HBM per device.

```python
import math
import jax
import jax.numpy as jnp
from jax import lax

CH = 128
HEIGHT = 64
WIDTH = 16
DEPTH = 16
SAMPLES = 2
PARAMS = 442368


def levels(rng, extent, shards, least, top_value):
    def one(axis_at, parts):
        draws = jax.random.uniform(jax.random.fold_in(jax.random.fold_in(rng, 6), axis_at), (parts,), jnp.float32, least / len(shards), top_value / len(shards))
        return jnp.repeat(jnp.exp(draws), extent[axis_at] // parts).reshape((-1,) + (1,) * (len(extent) - axis_at - 1))

    level = one(*shards[0])
    for cut in shards[1:]:
        level = level * one(*cut)
    return level


def bell_draw(stream_key, shape, scale, limit, shards=(), kind=jnp.bfloat16):
    entries = jax.random.normal(stream_key, shape, jnp.float32) * scale
    if len(shards) > 0:
        entries = levels(stream_key, shape, shards, -0.22, 0.18) * entries
    return jnp.clip(entries, min=-limit, max=limit).astype(kind)


def setup_inputs(seed: int = 0) -> dict:
    keys = jax.random.split(jax.random.key(seed), 8)
    activations = bell_draw(keys[0], (SAMPLES, DEPTH, HEIGHT, WIDTH, CH), 1.0, 6.0, ((0, 2), (1, 16)))
    preact = bell_draw(keys[1], (SAMPLES, DEPTH, HEIGHT, WIDTH, CH), 1.0, 6.0, ((0, 2), (1, 16)))
    out_grad = bell_draw(keys[2], (SAMPLES, DEPTH, HEIGHT, WIDTH, CH), 1.0, 6.0, ((0, 2), (1, 16)))
    weights = bell_draw(keys[3], (3, 3, 3, CH, CH), (27 * CH) ** -0.5, 0.109375)
    master = bell_draw(keys[4], (PARAMS,), (27 * CH) ** -0.5, 0.109375, ((0, 32),), jnp.float32)
    moment = bell_draw(keys[5], (PARAMS,), 0.5, 4.0, ((0, 32),), jnp.float32)
    second = jnp.clip(jnp.exp(math.log(1.0) - 2.3025851 * jax.random.uniform(keys[6], (PARAMS,), jnp.float32) ** levels(keys[6], (PARAMS,), ((0, 32),), -0.2, 0.2)), 0.1, 1.0)
    return dict(activations=activations, preact=preact, out_grad=out_grad, weights=weights, master=master, moment=moment, second=second)


first_fix = 1.0
second_fix = 0.63230457524

def reference(activations, preact, out_grad, weights, master, moment, second):
    planes = activations.shape[1]
    height = activations.shape[2]
    width = activations.shape[3]
    chans = activations.shape[4]
    count = activations.shape[0] * planes * height * width
    widths = ((1, 1), (1, 1), (1, 1), (0, 0))

    def per_sample(total, item):
        source, before, upstream = item
        slope = jnp.where(before > 0, jnp.float32(1.0), jnp.float32(0.01))
        cotangent = (upstream.astype(jnp.float32) * slope).astype(jnp.bfloat16)
        padded_cot = jnp.pad(cotangent, widths)
        padded_src = jnp.pad(source, widths)
        flat_cot = cotangent.reshape(-1, chans)
        result = jnp.zeros((planes * height * width, chans), jnp.float32)
        terms = []
        for depth_tap in range(3):
            for row_tap in range(3):
                for col_tap in range(3):
                    cot_part = padded_cot[2 - depth_tap:2 - depth_tap + planes, 2 - row_tap:2 - row_tap + height, 2 - col_tap:2 - col_tap + width]
                    result = result + jnp.dot(cot_part.reshape(-1, chans), weights[depth_tap, row_tap, col_tap].T, preferred_element_type=jnp.float32)
                    src_part = padded_src[depth_tap:depth_tap + planes, row_tap:row_tap + height, col_tap:col_tap + width]
                    terms.append(jnp.dot(src_part.reshape(-1, chans).T, flat_cot, preferred_element_type=jnp.float32))
        return (total + jnp.stack(terms), result.reshape(planes, height, width, chans).astype(jnp.bfloat16))
    start = jnp.zeros((27, chans, chans), jnp.float32)
    raw, grad_input = lax.scan(per_sample, start, (activations, preact, out_grad))
    filter_grad = raw.reshape(-1) * jnp.float32(1.0 / count ** 0.5)
    new_moment = 0.9 * moment + 0.1 * filter_grad
    new_second = 0.999 * second + 0.001 * filter_grad * filter_grad
    new_master = master - 0.01 * (new_moment / first_fix) / (jnp.sqrt(new_second / second_fix) + 1e-08)
    new_weights = new_master.astype(jnp.bfloat16).reshape(3, 3, 3, chans, chans)
    return (grad_input, filter_grad, new_moment, new_second, new_master, new_weights)
```

```python
import functools
import jax
import jax.numpy as jnp
from jax import lax
from jax.experimental import pallas as pl
from jax.experimental.pallas import tpu as pltpu
from jax.sharding import PartitionSpec as P

first_fix = 1.0
second_fix = 0.63230457524
AXES = ("depth", "samp")
VMEM = pl.BlockSpec(memory_space=pltpu.VMEM)
SMEM = pl.BlockSpec(memory_space=pltpu.SMEM)


def call(body, outs, n_in, flops=0, moved=0, scratch=(), limit=24 << 20):
    return pl.pallas_call(
        body,
        out_shape=outs,
        in_specs=[SMEM] + [VMEM] * n_in,
        out_specs=jax.tree.map(lambda _: VMEM, outs),
        scratch_shapes=list(scratch),
        cost_estimate=pl.CostEstimate(flops=flops, bytes_accessed=moved, transcendentals=0),
        compiler_params=pltpu.CompilerParams(vmem_limit_bytes=limit),
    )


def fill_shifted(shifted, slot, plane, width):
    rows, chans = plane.shape
    wide = plane.astype(jnp.float32)
    column = lax.broadcasted_iota(jnp.int32, (rows, chans), 0) % width
    nxt = jnp.where(column == width - 1, 0.0, pltpu.roll(wide, rows - 1, 0))
    prv = jnp.where(column == 0, 0.0, pltpu.roll(wide, 1, 0))
    edge = jnp.zeros((width, 3 * chans), plane.dtype)
    shifted[slot, 0:width, :] = edge
    shifted[slot, width + rows : 2 * width + rows, :] = edge
    body = slice(width, width + rows)
    shifted[slot, body, 0:chans] = nxt.astype(plane.dtype)
    shifted[slot, body, chans : 2 * chans] = plane
    shifted[slot, body, 2 * chans :] = prv.astype(plane.dtype)


def filter_body(width, pieces, step, me, act, cot, before, after, keep, send, shifted, grads):
    rows, chans = cot.shape
    left = act[...]
    for slot, plane in ((1, cot), (0, after), (2, before)):
        fill_shifted(shifted, slot, plane[...], width)
        for b in range(3):
            part = shifted[slot, (2 - b) * width : (2 - b) * width + rows, :]
            out = lax.dot_general(
                left, part, (((0,), (0,)), ((), ())), preferred_element_type=jnp.float32
            )
            for c in range(3):
                tap = (slot * 3 + b) * 3 + c
                grads[tap * chans : (tap + 1) * chans, :] = out[:, c * chans : (c + 1) * chans]
    chip = grads.shape[0] // pieces
    wide = keep.shape[1]
    mine = me[0] * step
    other = (1 - me[0]) * step
    for k in range(pieces):
        keep[k] = grads[pl.ds(pl.multiple_of(k * chip + mine, 8), wide), :]
        send[k] = grads[pl.ds(pl.multiple_of(k * chip + other, 8), wide), :]


def all_filter_body(width, me, act, cot, before, after, grads, shifted):
    rows, chans = cot.shape
    left = act[...]
    for slot, plane in ((1, cot), (0, after), (2, before)):
        fill_shifted(shifted, slot, plane[...], width)
        for b in range(3):
            part = shifted[slot, (2 - b) * width : (2 - b) * width + rows, :]
            out = lax.dot_general(
                left, part, (((0,), (0,)), ((), ())), preferred_element_type=jnp.float32
            )
            for c in range(3):
                tap = (slot * 3 + b) * 3 + c
                grads[tap * chans : (tap + 1) * chans, :] = out[:, c * chans : (c + 1) * chans]


def input_body(width, me, cot, before, after, weights, out, shifted):
    rows, chans = cot.shape
    total = jnp.zeros((rows, chans), jnp.float32)
    for slot, plane in ((1, cot), (0, after), (2, before)):
        fill_shifted(shifted, slot, plane[...], width)
        for b in range(3):
            part = shifted[slot, (2 - b) * width : (2 - b) * width + rows, :]
            taps = [weights[(slot * 3 + b) * 3 + c] for c in range(3)]
            total = total + lax.dot_general(
                part,
                jnp.concatenate(taps, axis=1),
                (((1,), (1,)), ((), ())),
                preferred_element_type=jnp.float32,
            )
    out[...] = total.astype(out.dtype)


def merge_body(n, me, *refs):
    terms, outs = refs[: len(refs) - n], refs[len(refs) - n :]
    place = me[0]
    for m in range(n):
        at = place ^ m
        for z in range(outs[m].shape[0]):
            total = terms[0][z * n + at]
            for term in terms[1:]:
                total = total + term[z * n + at]
            outs[m][z] = total


def adam_body(step, count, me, *refs):
    terms, (master, moment, second), outs = refs[:-8], refs[-8:-5], refs[-5:]
    total = terms[0][0]
    for term in terms[1:]:
        total = total + term[0]
    size = master.shape[0]
    skip = total.shape[0] - size
    raw = jnp.where(me[0] == 0, total[0:size], total[skip : skip + size])
    grad = raw * jnp.float32(1.0 / count**0.5)
    new_moment = 0.9 * moment[...] + 0.1 * grad
    new_second = 0.999 * second[...] + 0.001 * grad * grad
    new_master = master[...] - 0.01 * (new_moment / first_fix) / (
        jnp.sqrt(new_second / second_fix) + 1e-08
    )
    outs[0][...] = grad
    outs[1][...] = new_moment
    outs[2][...] = new_second
    outs[3][...] = new_master
    outs[4][0, 0:size, :] = new_master.astype(jnp.bfloat16)
    outs[4][0, size:, :] = jnp.zeros((outs[4].shape[1] - size, master.shape[1]), jnp.bfloat16)


def gather_body(me, *refs):
    for k, ref in enumerate(refs[:-1]):
        refs[-1][k] = ref[0]


def place_body(fast, slow, size, me, *refs):
    own, peer, out, held, wide = refs[:fast], refs[fast : 2 * fast], refs[-3], refs[-2], refs[-1]
    for m in range(fast):
        held[0, m] = own[m][...]
        held[1, m] = peer[m][...]
    for z in range(slow):
        for k in range(fast):
            for c in range(2):
                block = held[c ^ me[2], k ^ me[1], z ^ me[0]]
                at = ((z * fast + k) * 2 + c) * size
                wide[at : at + size, :] = block[0:size].astype(jnp.float32)
    out[...] = wide[...].astype(out.dtype)


def swap(array, axis, mask):
    return lax.ppermute(array, axis, [(i, i ^ mask) for i in range(lax.axis_size(axis))])


def staged(groups, act, cot, before, after, weights, states, width, count):
    fast, slow = groups
    chans = act.shape[1]
    rows = 27 * chans
    size = rows // (2 * fast * slow)
    chip = 2 * size
    wide = -(-size // 16) * 16
    step = chip - wide
    core, depth = lax.axis_index("samp"), lax.axis_index("depth")
    one = lambda value: jnp.reshape(value, (1,)).astype(jnp.int32)
    fast_at, slow_at = depth % fast, depth // fast
    f32 = lambda *shape: jax.ShapeDtypeStruct(shape, jnp.float32)
    b16 = lambda *shape: jax.ShapeDtypeStruct(shape, jnp.bfloat16)
    pieces = fast * slow
    shift_rows = cot.shape[0] + 2 * width
    half = f32(pieces, wide, chans)
    keep, send = call(
        functools.partial(filter_body, width, pieces, step),
        (half, half),
        4,
        flops=2 * rows * chans * cot.shape[0],
        scratch=[
            pltpu.VMEM((3, shift_rows, 3 * chans), jnp.bfloat16),
            pltpu.VMEM((rows, chans), jnp.float32),
        ],
    )(one(core), act, cot, before, after)
    come = swap(send, "samp", 1)
    parts = call(functools.partial(merge_body, fast), (f32(slow, wide, chans),) * fast, 2)(
        one(fast_at), keep, come
    )
    got = [parts[0]] + [swap(parts[m], "depth", m) for m in range(1, fast)]
    parts = call(functools.partial(merge_body, slow), (f32(1, wide, chans),) * slow, fast)(
        one(slow_at), *got
    )
    got = [parts[0]] + [swap(parts[m], "depth", m * fast) for m in range(1, slow)]
    grad_input = call(
        functools.partial(input_body, width),
        b16(*cot.shape),
        4,
        flops=2 * rows * chans * cot.shape[0],
        moved=4 << 20,
        scratch=[pltpu.VMEM((3, shift_rows, 3 * chans), jnp.bfloat16)],
    )(one(core), cot, before, after, weights)
    flat = f32(size, chans)
    states = [s.reshape(size, chans) for s in states]
    *fresh, share = call(
        functools.partial(adam_body, step, count), (flat,) * 4 + (b16(1, wide, chans),), slow + 3
    )(one(core), *got, *states)
    got = [share] + [swap(share, "depth", m * fast) for m in range(1, slow)]
    line = call(gather_body, b16(slow, wide, chans), slow)(one(core), *got)
    own = [line] + [swap(line, "depth", m) for m in range(1, fast)]
    peer = [swap(block, "samp", 1) for block in own]
    new_weights = call(
        functools.partial(place_body, fast, slow, size),
        b16(rows, chans),
        2 * fast,
        scratch=[
            pltpu.VMEM((2, fast, slow, wide, chans), jnp.bfloat16),
            pltpu.VMEM((rows, chans), jnp.float32),
        ],
    )(jnp.stack([slow_at, fast_at, core]).astype(jnp.int32), *own, *peer)
    return grad_input, [x.reshape(-1) for x in fresh], new_weights


def plain(act, cot, before, after, weights, states, width, count):
    chans = act.shape[1]
    rows = 27 * chans
    shift = pltpu.VMEM((3, cot.shape[0] + 2 * width, 3 * chans), jnp.bfloat16)
    core = jnp.reshape(lax.axis_index("samp"), (1,)).astype(jnp.int32)
    grads = call(
        functools.partial(all_filter_body, width),
        jax.ShapeDtypeStruct((rows, chans), jnp.float32),
        4,
        scratch=[shift],
    )(core, act, cot, before, after)
    grad_input = call(
        functools.partial(input_body, width),
        jax.ShapeDtypeStruct(cot.shape, jnp.bfloat16),
        4,
        scratch=[shift],
    )(core, cot, before, after, weights)
    total = lax.psum_scatter(grads.reshape(-1), AXES, scatter_dimension=0, tiled=True)
    master, moment, second = states
    grad = total * jnp.float32(1.0 / count**0.5)
    new_moment = 0.9 * moment + 0.1 * grad
    new_second = 0.999 * second + 0.001 * grad * grad
    new_master = master - 0.01 * (new_moment / first_fix) / (
        jnp.sqrt(new_second / second_fix) + 1e-08
    )
    whole = lax.all_gather(new_master.astype(jnp.bfloat16), AXES, axis=0, tiled=True)
    return grad_input, [grad, new_moment, new_second, new_master], whole


def local(groups, activations, preact, out_grad, weights, master, moment, second):
    samples, planes, height, width, chans = activations.shape
    count = samples * lax.axis_size("samp") * planes * lax.axis_size("depth") * height * width
    peers = lax.axis_size("depth")
    slope = jnp.where(preact > 0, jnp.float32(1.0), jnp.float32(0.01))
    cot = (out_grad.astype(jnp.float32) * slope).astype(jnp.bfloat16).reshape(-1, chans)
    act = activations.reshape(-1, chans)
    up = [(i, i + 1) for i in range(peers - 1)]
    before = lax.ppermute(cot, "depth", up)
    after = lax.ppermute(cot, "depth", [(j, i) for i, j in up])
    taps = weights.reshape(27, chans, chans)
    states = (master, moment, second)
    if groups:
        result = staged(groups, act, cot, before, after, taps, states, width, count)
    else:
        result = plain(act, cot, before, after, taps, states, width, count)
    grad_input, fresh, whole = result
    return (grad_input.reshape(activations.shape), *fresh, whole.reshape(weights.shape))


def stages(mesh):
    depth, samp = mesh.shape["depth"], mesh.shape["samp"]
    slow = 1
    while slow * slow < depth:
        slow *= 2
    if samp != 2 or slow * slow != depth:
        return None
    return depth // slow, slow


def solution(mesh):
    split = P("samp", "depth", None, None, None)
    shard = P(AXES)
    return jax.shard_map(
        functools.partial(local, stages(mesh)),
        mesh=mesh,
        in_specs=(split, split, split, P(), shard, shard, shard),
        out_specs=(split, shard, shard, shard, shard, P()),
        check_vma=False,
    )
```

```python
import functools
import math
import jax
import jax.numpy as jnp
from jax import lax
from jax.experimental import pallas as pl
from jax.experimental.pallas import tpu as pltpu
from jax.sharding import PartitionSpec as P

first_fix = 1.0
second_fix = 0.63230457524
AXES = ("depth", "samp")
VMEM = pl.BlockSpec(memory_space=pltpu.VMEM)
SMEM = pl.BlockSpec(memory_space=pltpu.SMEM)


def call(body, outs, n_in, flops=0, moved=0, scratch=(), limit=8 << 20, scalars=1):
    return pl.pallas_call(
        body,
        out_shape=outs,
        in_specs=[SMEM] * scalars + [VMEM] * n_in,
        out_specs=jax.tree.map(lambda _: VMEM, outs),
        scratch_shapes=list(scratch),
        cost_estimate=pl.CostEstimate(flops=flops, bytes_accessed=moved, transcendentals=0),
        compiler_params=pltpu.CompilerParams(vmem_limit_bytes=limit),
    )


def fill_shifted(shifted, slot, plane, width):
    rows, chans = plane.shape
    wide = plane.astype(jnp.float32)
    column = lax.broadcasted_iota(jnp.int32, (rows, chans), 0) % width
    nxt = jnp.where(column == width - 1, 0.0, pltpu.roll(wide, rows - 1, 0))
    prv = jnp.where(column == 0, 0.0, pltpu.roll(wide, 1, 0))
    edge = jnp.zeros((width, 3 * chans), plane.dtype)
    shifted[slot, 0:width, :] = edge
    shifted[slot, width + rows : 2 * width + rows, :] = edge
    body = slice(width, width + rows)
    shifted[slot, body, 0:chans] = nxt.astype(plane.dtype)
    shifted[slot, body, chans : 2 * chans] = plane
    shifted[slot, body, 2 * chans :] = prv.astype(plane.dtype)


def filter_body(width, pieces, step, me, act, cot, before, after, keep, send, shifted, grads):
    rows, chans = cot.shape
    left = act[...]
    for slot, plane in ((1, cot), (0, after), (2, before)):
        fill_shifted(shifted, slot, plane[...], width)
        for b in range(3):
            part = shifted[slot, (2 - b) * width : (2 - b) * width + rows, :]
            out = lax.dot_general(
                left, part, (((0,), (0,)), ((), ())), preferred_element_type=jnp.float32
            )
            for c in range(3):
                tap = (slot * 3 + b) * 3 + c
                grads[tap * chans : (tap + 1) * chans, :] = out[:, c * chans : (c + 1) * chans]
    chip = grads.shape[0] // pieces
    wide = keep.shape[1]
    mine = me[0] * step
    other = (1 - me[0]) * step
    for k in range(pieces):
        keep[k] = grads[pl.ds(pl.multiple_of(k * chip + mine, 8), wide), :]
        send[k] = grads[pl.ds(pl.multiple_of(k * chip + other, 8), wide), :]


def all_filter_body(width, me, act, cot, before, after, grads, shifted):
    rows, chans = cot.shape
    left = act[...]
    for slot, plane in ((1, cot), (0, after), (2, before)):
        fill_shifted(shifted, slot, plane[...], width)
        for b in range(3):
            part = shifted[slot, (2 - b) * width : (2 - b) * width + rows, :]
            out = lax.dot_general(
                left, part, (((0,), (0,)), ((), ())), preferred_element_type=jnp.float32
            )
            for c in range(3):
                tap = (slot * 3 + b) * 3 + c
                grads[tap * chans : (tap + 1) * chans, :] = out[:, c * chans : (c + 1) * chans]


def input_body(width, me, cot, before, after, weights, out, token, shifted):
    rows, chans = cot.shape
    total = jnp.zeros((rows, chans), jnp.float32)
    for slot, plane in ((1, cot), (0, after), (2, before)):
        fill_shifted(shifted, slot, plane[...], width)
        for b in range(3):
            part = shifted[slot, (2 - b) * width : (2 - b) * width + rows, :]
            taps = [weights[(slot * 3 + b) * 3 + c] for c in range(3)]
            total = total + lax.dot_general(
                part,
                jnp.concatenate(taps, axis=1),
                (((1,), (1,)), ((), ())),
                preferred_element_type=jnp.float32,
            )
    out[...] = total.astype(out.dtype)
    token[...] = jnp.zeros(token.shape, token.dtype)


def merge_body(n, swapped, core, first, second, *refs):
    outs = refs[len(refs) - n :]
    terms = [r for r in refs[: len(refs) - n] if len(r.shape) == 3]
    flip = core[0] != swapped
    own = jnp.where(flip, second[0], first[0])
    group, other = jnp.where(flip, n, 1), jnp.where(flip, 1, n)
    for j in range(n):
        at = own ^ j
        for h in range(outs[j].shape[0]):
            piece = at * group + h * other if outs[j].shape[0] > 1 else at
            total = terms[0][piece]
            for term in terms[1:]:
                total = total + term[piece]
            outs[j][h] = total


def adam_body(step, count, me, *refs):
    terms, (master, moment, second), outs = refs[:-8], refs[-8:-5], refs[-5:]
    total = terms[0][0]
    for term in terms[1:]:
        total = total + term[0]
    size = master.shape[0]
    skip = total.shape[0] - size
    raw = jnp.where(me[0] == 0, total[0:size], total[skip : skip + size])
    grad = raw * jnp.float32(1.0 / count**0.5)
    new_moment = 0.9 * moment[...] + 0.1 * grad
    new_second = 0.999 * second[...] + 0.001 * grad * grad
    new_master = master[...] - 0.01 * (new_moment / first_fix) / (
        jnp.sqrt(new_second / second_fix) + 1e-08
    )
    outs[0][...] = grad
    outs[1][...] = new_moment
    outs[2][...] = new_second
    outs[3][...] = new_master
    outs[4][0, 0:size, :] = new_master.astype(jnp.bfloat16)
    outs[4][0, size:, :] = jnp.zeros((outs[4].shape[1] - size, master.shape[1]), jnp.bfloat16)


def gather_body(me, *refs):
    for k, ref in enumerate(refs[:-1]):
        refs[-1][k] = ref[0]


def place_body(n, size, core, first, second, *refs):
    own, peer, out, held, wide = refs[:n], refs[n : 2 * n], refs[-3], refs[-2], refs[-1]
    for m in range(n):
        held[0, m] = own[m][...]
        held[1, m] = peer[m][...]
    for z in range(n):
        for k in range(n):
            for c in range(2):
                block = held[c ^ core[0], k ^ first[0], z ^ second[0]]
                at = ((z * n + k) * 2 + c) * size
                wide[at : at + size, :] = block[0:size].astype(jnp.float32)
    out[...] = wide[...].astype(out.dtype)


def swap(array, even, odd=None):
    masks = (even, even if odd is None else odd)
    peers = lax.axis_size("depth")
    pairs = [(2 * d + c, 2 * (d ^ masks[c]) + c) for d in range(peers) for c in range(2)]
    return lax.ppermute(array, AXES, pairs)


def swap_cores(array):
    return lax.ppermute(array, "samp", [(0, 1), (1, 0)])


def staged(n, act, cot, before, after, weights, states, width, count):
    chans = act.shape[1]
    rows = 27 * chans
    pieces = n * n
    size = rows // (2 * pieces)
    wide = -(-size // 16) * 16
    step = 2 * size - wide
    depth = lax.axis_index("depth")
    one = lambda value: jnp.reshape(value, (1,)).astype(jnp.int32)
    core, first, second = one(lax.axis_index("samp")), one(depth % n), one(depth // n)
    f32 = lambda *shape: jax.ShapeDtypeStruct(shape, jnp.float32)
    b16 = lambda *shape: jax.ShapeDtypeStruct(shape, jnp.bfloat16)
    shift = pltpu.VMEM((3, cot.shape[0] + 2 * width, 3 * chans), jnp.bfloat16)
    flops = 2 * rows * chans * cot.shape[0]
    keep, send = call(
        functools.partial(filter_body, width, pieces, step),
        (f32(pieces, wide, chans),) * 2,
        4,
        flops=flops,
        scratch=[shift, pltpu.VMEM((rows, chans), jnp.float32)],
        limit=16 << 20,
    )(core, act, cot, before, after)
    come = swap_cores(send)
    parts = call(
        functools.partial(merge_body, n, 0), (f32(n, wide, chans),) * n, 2, scalars=3
    )(core, first, second, keep, come)
    got = [parts[0]] + [swap(parts[m], m, m * n) for m in range(1, n)]
    grad_input, token = call(
        functools.partial(input_body, width),
        (b16(*cot.shape), f32(8, chans)),
        4,
        flops=flops,
        moved=4 << 20,
        scratch=[shift],
        limit=16 << 20,
    )(core, cot, before, after, weights)
    parts = call(
        functools.partial(merge_body, n, 1),
        (f32(1, wide, chans),) * n,
        n + 1,
        scalars=3,
    )(core, first, second, *got, token)
    got = [parts[0]] + [swap(parts[m], m * n, m) for m in range(1, n)]
    states = [s.reshape(size, chans) for s in states]
    *fresh, share = call(
        functools.partial(adam_body, step, count),
        (f32(size, chans),) * 4 + (b16(1, wide, chans),),
        n + 3,
    )(core, *got, *states)
    got = [share] + [swap(share, m * n) for m in range(1, n)]
    line = call(gather_body, b16(n, wide, chans), n)(core, *got)
    own = [line] + [swap(line, m) for m in range(1, n)]
    peer = [swap_cores(block) for block in own]
    new_weights = call(
        functools.partial(place_body, n, size),
        b16(rows, chans),
        2 * n,
        scratch=[
            pltpu.VMEM((2, n, n, wide, chans), jnp.bfloat16),
            pltpu.VMEM((rows, chans), jnp.float32),
        ],
        scalars=3,
    )(core, first, second, *own, *peer)
    return grad_input, [x.reshape(-1) for x in fresh], new_weights


def plain(act, cot, before, after, weights, states, width, count):
    chans = act.shape[1]
    rows = 27 * chans
    shift = pltpu.VMEM((3, cot.shape[0] + 2 * width, 3 * chans), jnp.bfloat16)
    core = jnp.reshape(lax.axis_index("samp"), (1,)).astype(jnp.int32)
    grads = call(
        functools.partial(all_filter_body, width),
        jax.ShapeDtypeStruct((rows, chans), jnp.float32),
        4,
        scratch=[shift],
        limit=16 << 20,
    )(core, act, cot, before, after)
    grad_input, _ = call(
        functools.partial(input_body, width),
        (
            jax.ShapeDtypeStruct(cot.shape, jnp.bfloat16),
            jax.ShapeDtypeStruct((8, chans), jnp.float32),
        ),
        4,
        scratch=[shift],
        limit=16 << 20,
    )(core, cot, before, after, weights)
    total = lax.psum_scatter(grads.reshape(-1), AXES, scatter_dimension=0, tiled=True)
    master, moment, second = states
    grad = total * jnp.float32(1.0 / count**0.5)
    new_moment = 0.9 * moment + 0.1 * grad
    new_second = 0.999 * second + 0.001 * grad * grad
    new_master = master - 0.01 * (new_moment / first_fix) / (
        jnp.sqrt(new_second / second_fix) + 1e-08
    )
    whole = lax.all_gather(new_master.astype(jnp.bfloat16), AXES, axis=0, tiled=True)
    return grad_input, [grad, new_moment, new_second, new_master], whole


def local(n, activations, preact, out_grad, weights, master, moment, second):
    samples, planes, height, width, chans = activations.shape
    count = samples * lax.axis_size("samp") * planes * lax.axis_size("depth") * height * width
    peers = lax.axis_size("depth")
    slope = jnp.where(preact > 0, jnp.float32(1.0), jnp.float32(0.01))
    cot = (out_grad.astype(jnp.float32) * slope).astype(jnp.bfloat16).reshape(-1, chans)
    act = activations.reshape(-1, chans)
    up = [(i, i + 1) for i in range(peers - 1)]
    before = lax.ppermute(cot, "depth", up)
    after = lax.ppermute(cot, "depth", [(j, i) for i, j in up])
    taps = weights.reshape(27, chans, chans)
    states = (master, moment, second)
    if n:
        result = staged(n, act, cot, before, after, taps, states, width, count)
    else:
        result = plain(act, cot, before, after, taps, states, width, count)
    grad_input, fresh, whole = result
    return (grad_input.reshape(activations.shape), *fresh, whole.reshape(weights.shape))


def stages(mesh):
    n = math.isqrt(mesh.shape["depth"])
    ready = mesh.shape["samp"] == 2 and n * n == mesh.shape["depth"] and n & (n - 1) == 0
    return n if ready else 0


def solution(mesh):
    split = P("samp", "depth", None, None, None)
    shard = P(AXES)
    return jax.shard_map(
        functools.partial(local, stages(mesh)),
        mesh=mesh,
        in_specs=(split, split, split, P(), shard, shard, shard),
        out_specs=(split, shard, shard, shard, shard, P()),
        check_vma=False,
    )
```

```python
import functools
import math
import jax
import jax.numpy as jnp
from jax import lax
from jax.experimental import pallas as pl
from jax.experimental.pallas import tpu as pltpu
from jax.sharding import PartitionSpec as P

first_fix = 1.0
second_fix = 0.63230457524
AXES = ("depth", "samp")
VMEM = pl.BlockSpec(memory_space=pltpu.VMEM)
SMEM = pl.BlockSpec(memory_space=pltpu.SMEM)


def call(body, outs, n_in, flops=0, moved=0, scratch=(), limit=8 << 20, scalars=1):
    return pl.pallas_call(
        body,
        out_shape=outs,
        in_specs=[SMEM] * scalars + [VMEM] * n_in,
        out_specs=jax.tree.map(lambda _: VMEM, outs),
        scratch_shapes=list(scratch),
        cost_estimate=pl.CostEstimate(flops=flops, bytes_accessed=moved, transcendentals=0),
        compiler_params=pltpu.CompilerParams(vmem_limit_bytes=limit),
    )


def fill_shifted(shifted, slot, halves, width):
    plane = jnp.concatenate([half[...] for half in halves], axis=0)
    rows, chans = plane.shape
    wide = plane.astype(jnp.float32)
    column = lax.broadcasted_iota(jnp.int32, (rows, chans), 0) % width
    nxt = jnp.where(column == width - 1, 0.0, pltpu.roll(wide, rows - 1, 0))
    prv = jnp.where(column == 0, 0.0, pltpu.roll(wide, 1, 0))
    edge = jnp.zeros((width, 3 * chans), plane.dtype)
    shifted[slot, 0:width, :] = edge
    shifted[slot, width + rows : 2 * width + rows, :] = edge
    body = slice(width, width + rows)
    shifted[slot, body, 0:chans] = nxt.astype(plane.dtype)
    shifted[slot, body, chans : 2 * chans] = plane
    shifted[slot, body, 2 * chans :] = prv.astype(plane.dtype)


def planes_of(odd, refs):
    yield 0, 1, refs[0:2]
    yield 1, 2 * odd, refs[2:4]
    yield 2, 2 - 2 * odd, refs[4:6]


def filter_taps(width, odd, act, halves, grads, shifted):
    left = act[...]
    rows, chans = left.shape
    for slot, deep, plane in planes_of(odd, halves):
        fill_shifted(shifted, slot, plane, width)
        for b in range(3):
            part = shifted[slot, (2 - b) * width : (2 - b) * width + rows, :]
            out = lax.dot_general(
                left, part, (((0,), (0,)), ((), ())), preferred_element_type=jnp.float32
            )
            for c in range(3):
                at = ((deep * 3 + b) * 3 + c) * chans
                if slot > 0:
                    at = pl.multiple_of(at, chans)
                grads[pl.ds(at, chans), :] = out[:, c * chans : (c + 1) * chans]


def filter_body(width, pieces, step, core, odd, act, *refs):
    halves, (keep, send, shifted, grads) = refs[:6], refs[6:]
    filter_taps(width, odd[0], act, halves, grads, shifted)
    chip = grads.shape[0] // pieces
    wide = keep.shape[1]
    mine = core[0] * step
    other = (1 - core[0]) * step
    for k in range(pieces):
        keep[k] = grads[pl.ds(pl.multiple_of(k * chip + mine, 8), wide), :]
        send[k] = grads[pl.ds(pl.multiple_of(k * chip + other, 8), wide), :]


def all_filter_body(width, odd, act, *refs):
    halves, (grads, shifted) = refs[:6], refs[6:]
    filter_taps(width, odd[0], act, halves, grads, shifted)


def input_body(width, odd, weights, *refs):
    halves, (out, token, shifted) = refs[:6], refs[6:]
    rows, chans = out.shape
    total = jnp.zeros((rows, chans), jnp.float32)
    for slot, deep, plane in planes_of(odd[0], halves):
        fill_shifted(shifted, slot, plane, width)
        for b in range(3):
            part = shifted[slot, (2 - b) * width : (2 - b) * width + rows, :]
            taps = [weights[(deep * 3 + b) * 3 + c] for c in range(3)]
            total = total + lax.dot_general(
                part,
                jnp.concatenate(taps, axis=1),
                (((1,), (1,)), ((), ())),
                preferred_element_type=jnp.float32,
            )
    out[...] = total.astype(out.dtype)
    token[...] = jnp.zeros(token.shape, token.dtype)


def merge_body(n, swapped, core, first, second, *refs):
    outs = refs[len(refs) - n :]
    terms = [r for r in refs[: len(refs) - n] if len(r.shape) == 3]
    flip = core[0] != swapped
    own = jnp.where(flip, second[0], first[0])
    group, other = jnp.where(flip, n, 1), jnp.where(flip, 1, n)
    for j in range(n):
        at = own ^ j
        for h in range(outs[j].shape[0]):
            piece = at * group + h * other if outs[j].shape[0] > 1 else at
            total = terms[0][piece]
            for term in terms[1:]:
                total = total + term[piece]
            outs[j][h] = total


def adam_body(step, count, me, *refs):
    terms, (master, moment, second), outs = refs[:-8], refs[-8:-5], refs[-5:]
    total = terms[0][0]
    for term in terms[1:]:
        total = total + term[0]
    size = master.shape[0]
    skip = total.shape[0] - size
    raw = jnp.where(me[0] == 0, total[0:size], total[skip : skip + size])
    grad = raw * jnp.float32(1.0 / count**0.5)
    new_moment = 0.9 * moment[...] + 0.1 * grad
    new_second = 0.999 * second[...] + 0.001 * grad * grad
    new_master = master[...] - 0.01 * (new_moment / first_fix) / (
        jnp.sqrt(new_second / second_fix) + 1e-08
    )
    outs[0][...] = grad
    outs[1][...] = new_moment
    outs[2][...] = new_second
    outs[3][...] = new_master
    outs[4][0, 0:size, :] = new_master.astype(jnp.bfloat16)
    outs[4][0, size:, :] = jnp.zeros((outs[4].shape[1] - size, master.shape[1]), jnp.bfloat16)


def gather_body(me, *refs):
    for k, ref in enumerate(refs[:-1]):
        refs[-1][k] = ref[0]


def place_body(n, size, core, first, second, *refs):
    own, peer, out, held, wide = refs[:n], refs[n : 2 * n], refs[-3], refs[-2], refs[-1]
    for m in range(n):
        held[0, m] = own[m][...]
        held[1, m] = peer[m][...]
    for z in range(n):
        for k in range(n):
            for c in range(2):
                block = held[c ^ core[0], k ^ first[0], z ^ second[0]]
                at = ((z * n + k) * 2 + c) * size
                wide[at : at + size, :] = block[0:size].astype(jnp.float32)
    out[...] = wide[...].astype(out.dtype)


def swap(array, even, odd=None):
    masks = (even, even if odd is None else odd)
    peers = lax.axis_size("depth")
    pairs = [(2 * d + c, 2 * (d ^ masks[c]) + c) for d in range(peers) for c in range(2)]
    return lax.ppermute(array, AXES, pairs)


def swap_cores(array):
    return lax.ppermute(array, "samp", [(0, 1), (1, 0)])


def staged(n, act, halves, odd, weights, states, width, count):
    chans = act.shape[1]
    rows = 27 * chans
    pieces = n * n
    size = rows // (2 * pieces)
    wide = -(-size // 16) * 16
    step = 2 * size - wide
    depth = lax.axis_index("depth")
    one = lambda value: jnp.reshape(value, (1,)).astype(jnp.int32)
    core, first, second = one(lax.axis_index("samp")), one(depth % n), one(depth // n)
    f32 = lambda *shape: jax.ShapeDtypeStruct(shape, jnp.float32)
    b16 = lambda *shape: jax.ShapeDtypeStruct(shape, jnp.bfloat16)
    shift = pltpu.VMEM((3, act.shape[0] + 2 * width, 3 * chans), jnp.bfloat16)
    flops = 2 * rows * chans * act.shape[0]
    keep, send = call(
        functools.partial(filter_body, width, pieces, step),
        (f32(pieces, wide, chans),) * 2,
        7,
        flops=flops,
        scratch=[shift, pltpu.VMEM((rows, chans), jnp.float32)],
        limit=16 << 20,
        scalars=2,
    )(core, odd, act, *halves)
    come = swap_cores(send)
    parts = call(
        functools.partial(merge_body, n, 0), (f32(n, wide, chans),) * n, 2, scalars=3
    )(core, first, second, keep, come)
    got = [parts[0]] + [swap(parts[m], m, m * n) for m in range(1, n)]
    grad_input, token = call(
        functools.partial(input_body, width),
        (b16(*act.shape), f32(8, chans)),
        7,
        flops=flops,
        moved=4 << 20,
        scratch=[shift],
        limit=16 << 20,
    )(odd, weights, *halves)
    parts = call(
        functools.partial(merge_body, n, 1),
        (f32(1, wide, chans),) * n,
        n + 1,
        scalars=3,
    )(core, first, second, *got, token)
    got = [parts[0]] + [swap(parts[m], m * n, m) for m in range(1, n)]
    states = [s.reshape(size, chans) for s in states]
    *fresh, share = call(
        functools.partial(adam_body, step, count),
        (f32(size, chans),) * 4 + (b16(1, wide, chans),),
        n + 3,
    )(core, *got, *states)
    got = [share] + [swap(share, m * n) for m in range(1, n)]
    line = call(gather_body, b16(n, wide, chans), n)(core, *got)
    own = [line] + [swap(line, m) for m in range(1, n)]
    peer = [swap_cores(block) for block in own]
    new_weights = call(
        functools.partial(place_body, n, size),
        b16(rows, chans),
        2 * n,
        scratch=[
            pltpu.VMEM((2, n, n, wide, chans), jnp.bfloat16),
            pltpu.VMEM((rows, chans), jnp.float32),
        ],
        scalars=3,
    )(core, first, second, *own, *peer)
    return grad_input, [x.reshape(-1) for x in fresh], new_weights


def plain(act, halves, odd, weights, states, width, count):
    chans = act.shape[1]
    rows = 27 * chans
    shift = pltpu.VMEM((3, act.shape[0] + 2 * width, 3 * chans), jnp.bfloat16)
    grads = call(
        functools.partial(all_filter_body, width),
        jax.ShapeDtypeStruct((rows, chans), jnp.float32),
        7,
        scratch=[shift],
        limit=16 << 20,
    )(odd, act, *halves)
    grad_input, _ = call(
        functools.partial(input_body, width),
        (
            jax.ShapeDtypeStruct(act.shape, jnp.bfloat16),
            jax.ShapeDtypeStruct((8, chans), jnp.float32),
        ),
        7,
        scratch=[shift],
        limit=16 << 20,
    )(odd, weights, *halves)
    total = lax.psum_scatter(grads.reshape(-1), AXES, scatter_dimension=0, tiled=True)
    master, moment, second = states
    grad = total * jnp.float32(1.0 / count**0.5)
    new_moment = 0.9 * moment + 0.1 * grad
    new_second = 0.999 * second + 0.001 * grad * grad
    new_master = master - 0.01 * (new_moment / first_fix) / (
        jnp.sqrt(new_second / second_fix) + 1e-08
    )
    whole = lax.all_gather(new_master.astype(jnp.bfloat16), AXES, axis=0, tiled=True)
    return grad_input, [grad, new_moment, new_second, new_master], whole


def neighbours(top, bottom):
    peers = lax.axis_size("depth")
    move = lambda array, pairs: lax.ppermute(array, "depth", pairs)
    partner = [(i, i ^ 1) for i in range(peers)]
    direct = [(i - 1, i) for i in range(2, peers, 2)] + [(i + 1, i) for i in range(1, peers - 1, 2)]
    relayed = [(i - 2, i) for i in range(2, peers, 2)] + [(i + 2, i) for i in range(1, peers - 1, 2)]
    partner_top, partner_bottom = move(top, partner), move(bottom, partner)
    other_bottom, other_top = move(bottom, direct), move(partner_top, relayed)
    return (top, bottom, partner_top, partner_bottom, other_top, other_bottom)


def local(n, activations, preact, out_grad, weights, master, moment, second):
    samples, planes, height, width, chans = activations.shape
    count = samples * lax.axis_size("samp") * planes * lax.axis_size("depth") * height * width
    act = activations.reshape(-1, chans)
    half = act.shape[0] // 2

    def cotangent(part):
        slope = jnp.where(preact.reshape(-1, chans)[part] > 0, jnp.float32(1.0), jnp.float32(0.01))
        return (out_grad.reshape(-1, chans)[part].astype(jnp.float32) * slope).astype(jnp.bfloat16)

    halves = neighbours(cotangent(slice(0, half)), cotangent(slice(half, None)))
    odd = jnp.reshape(lax.axis_index("depth") % 2, (1,)).astype(jnp.int32)
    taps = weights.reshape(27, chans, chans)
    states = (master, moment, second)
    if n:
        result = staged(n, act, halves, odd, taps, states, width, count)
    else:
        result = plain(act, halves, odd, taps, states, width, count)
    grad_input, fresh, whole = result
    return (grad_input.reshape(activations.shape), *fresh, whole.reshape(weights.shape))


def stages(mesh):
    n = math.isqrt(mesh.shape["depth"])
    ready = mesh.shape["samp"] == 2 and n * n == mesh.shape["depth"] and n & (n - 1) == 0
    return n if ready else 0


def solution(mesh):
    split = P("samp", "depth", None, None, None)
    shard = P(AXES)
    return jax.shard_map(
        functools.partial(local, stages(mesh)),
        mesh=mesh,
        in_specs=(split, split, split, P(), shard, shard, shard),
        out_specs=(split, shard, shard, shard, shard, P()),
        check_vma=False,
    )
```

```python
import functools
import math
import jax
import jax.numpy as jnp
from jax import lax
from jax.experimental import pallas as pl
from jax.experimental.pallas import tpu as pltpu
from jax.sharding import PartitionSpec as P

first_fix = 1.0
second_fix = 0.63230457524
AXES = ("depth", "samp")
VMEM = pl.BlockSpec(memory_space=pltpu.VMEM)
SMEM = pl.BlockSpec(memory_space=pltpu.SMEM)


def call(body, outs, n_in, flops=0, moved=0, scratch=(), limit=2 << 20, scalars=1, spec=VMEM):
    return pl.pallas_call(
        body,
        out_shape=outs,
        in_specs=[SMEM] * scalars + [VMEM] * n_in,
        out_specs=jax.tree.map(lambda _: spec, outs),
        scratch_shapes=list(scratch),
        cost_estimate=pl.CostEstimate(flops=flops, bytes_accessed=moved, transcendentals=0),
        compiler_params=pltpu.CompilerParams(vmem_limit_bytes=limit),
    )


def fill_shifted(shifted, slot, halves, width):
    plane = jnp.concatenate([half[...] for half in halves], axis=0)
    rows, chans = plane.shape
    wide = plane.astype(jnp.float32)
    column = lax.broadcasted_iota(jnp.int32, (rows, chans), 0) % width
    nxt = jnp.where(column == width - 1, 0.0, pltpu.roll(wide, rows - 1, 0))
    prv = jnp.where(column == 0, 0.0, pltpu.roll(wide, 1, 0))
    edge = jnp.zeros((width, 3 * chans), plane.dtype)
    shifted[slot, 0:width, :] = edge
    shifted[slot, width + rows : 2 * width + rows, :] = edge
    body = slice(width, width + rows)
    shifted[slot, body, 0:chans] = nxt.astype(plane.dtype)
    shifted[slot, body, chans : 2 * chans] = plane
    shifted[slot, body, 2 * chans :] = prv.astype(plane.dtype)


def planes_of(odd, refs):
    yield 0, 1, refs[0:2]
    yield 1, 2 * odd, refs[2:4]
    yield 2, 2 - 2 * odd, refs[4:6]


def filter_taps(width, act, planes, grads, shifted, base=0):
    left = act[...]
    rows, chans = left.shape
    for slot, deep, plane in planes:
        fill_shifted(shifted, slot, plane, width)
        for b in range(3):
            part = shifted[slot, (2 - b) * width : (2 - b) * width + rows, :]
            out = lax.dot_general(
                left, part, (((0,), (0,)), ((), ())), preferred_element_type=jnp.float32
            )
            for c in range(3):
                at = ((deep * 3 + b) * 3 + c) * chans - base
                if not isinstance(at, int):
                    at = pl.multiple_of(at, chans)
                grads[pl.ds(at, chans), :] = out[:, c * chans : (c + 1) * chans]


def pick(source, keep, send, core, step, pairs):
    wide = keep.shape[1]
    for at, kept, sent in pairs:
        keep[kept] = source[pl.ds(pl.multiple_of(at + core * step, 8), wide), :]
        send[sent] = source[pl.ds(pl.multiple_of(at + (1 - core) * step, 8), wide), :]


def early_body(width, chip, first, step, core, act, top, bottom, edges, keep, send, shifted, grads):
    base = grads.shape[0]
    filter_taps(width, act, [(0, 1, (top, bottom))], grads, shifted, base)
    count = keep.shape[0]
    pairs = [((first + k) * chip - base, k, k) for k in range(count)]
    pick(grads, keep, send, core[0], step, pairs)
    lead, tail = first * chip - base, (first + count) * chip - base
    edges[0:lead, :] = grads[0:lead, :]
    edges[lead:, :] = grads[tail:, :]


def late_body(width, chip, first, step, core, odd, act, *refs):
    halves, edges, (keep, send, shifted, grads) = refs[:4], refs[4], refs[6:]
    base = grads.shape[0] // 3
    total = grads.shape[0] // chip
    last = first + total - keep.shape[0]
    lead = first * chip - base
    grads[base : first * chip, :] = edges[0:lead, :]
    grads[last * chip : 2 * base, :] = edges[lead:, :]
    filter_taps(width, act, list(planes_of(odd[0], (None, None, *halves)))[1:], grads, shifted)
    pieces = [k for k in range(total) if k < first or k >= last]
    pick(grads, keep, send, core[0], step, [(k * chip, j, j) for j, k in enumerate(pieces)])


def all_filter_body(width, odd, act, *refs):
    halves, (grads, shifted) = refs[:6], refs[6:]
    filter_taps(width, act, planes_of(odd[0], halves), grads, shifted)


def input_body(width, odd, weights, *refs):
    halves, (out, token, shifted) = refs[:6], refs[6:]
    rows, chans = out.shape
    total = jnp.zeros((rows, chans), jnp.float32)
    for slot, deep, plane in planes_of(odd[0], halves):
        fill_shifted(shifted, slot, plane, width)
        for b in range(3):
            part = shifted[slot, (2 - b) * width : (2 - b) * width + rows, :]
            taps = [weights[(deep * 3 + b) * 3 + c] for c in range(3)]
            total = total + lax.dot_general(
                part,
                jnp.concatenate(taps, axis=1),
                (((1,), (1,)), ((), ())),
                preferred_element_type=jnp.float32,
            )
    out[...] = total.astype(out.dtype)
    token[...] = jnp.zeros(token.shape, token.dtype)


def merge_body(n, swapped, early, core, first, second, *refs):
    outs = refs[len(refs) - n :]
    terms = [r for r in refs[: len(refs) - n] if len(r.shape) == 3]
    flip = core[0] != swapped
    own = jnp.where(flip, second[0], first[0])
    group, other = jnp.where(flip, n, 1), jnp.where(flip, 1, n)
    add = lambda some, at: functools.reduce(lambda x, y: x + y, [term[at] for term in some])
    for j in range(n):
        at = own ^ j
        for h in range(outs[j].shape[0]):
            piece = at * group + h * other if outs[j].shape[0] > 1 else at
            if early is None:
                outs[j][h] = add(terms, piece)
                continue
            run = terms[-1].shape[0]
            inside = jnp.clip(piece - early, 0, run - 1)
            outside = jnp.clip(piece - jnp.where(piece >= early, run, 0), 0, terms[0].shape[0] - 1)
            within = (piece >= early) & (piece < early + run)
            outs[j][h] = jnp.where(within, add(terms[-2:], inside), add(terms[:-2], outside))


def adam_step(count, core, terms, master, moment, second):
    total = terms[0][0]
    for term in terms[1:]:
        total = total + term[0]
    size = master.shape[0]
    skip = total.shape[0] - size
    raw = jnp.where(core == 0, total[0:size], total[skip : skip + size])
    grad = raw * jnp.float32(1.0 / count**0.5)
    new_moment = 0.9 * moment[...] + 0.1 * grad
    new_second = 0.999 * second[...] + 0.001 * grad * grad
    new_master = master[...] - 0.01 * (new_moment / first_fix) / (
        jnp.sqrt(new_second / second_fix) + 1e-08
    )
    return grad, new_moment, new_second, new_master


def share_body(count, core, *refs):
    terms, (master, moment, second, share) = refs[:-4], refs[-4:]
    size, chans = master.shape
    new_master = adam_step(count, core[0], terms, master, moment, second)[3]
    share[0, 0:size, :] = new_master.astype(share.dtype)
    share[0, size:, :] = jnp.zeros((share.shape[1] - size, chans), share.dtype)


def adam_body(count, core, *refs):
    terms, (master, moment, second, _), outs = refs[:-9], refs[-9:-5], refs[-5:]
    for out, value in zip(outs, adam_step(count, core[0], terms, master, moment, second)):
        out[...] = value
    outs[4][...] = jnp.zeros(outs[4].shape, outs[4].dtype)


def gather_body(me, *refs):
    blocks = [r for r in refs[:-1] if len(r.shape) == 3]
    for k, ref in enumerate(blocks):
        refs[-1][k] = ref[0]


def place_body(n, size, core, first, second, *refs):
    own, peer, (out, wide, done, sems) = refs[:n], refs[n : 2 * n], refs[2 * n :]
    chunk = 4 * size
    flip, other = (first[0] & 1) == 1, core[0] == 1
    copies = []
    for z in range(n):
        for k in range(0, n, 2):
            for low in range(2):
                for c in range(2):
                    here = jnp.where(flip, own[k + 1 - low][z], own[k + low][z])
                    there = jnp.where(flip, peer[k + 1 - low][z], peer[k + low][z])
                    block = jnp.where(other, here, there) if c else jnp.where(other, there, here)
                    at = (2 * low + c) * size
                    wide[at : at + size, :] = block[0:size].astype(jnp.float32)
            step = len(copies)
            done[step] = wide[...].astype(done.dtype)
            to = (z ^ second[0]) * (n // 2) + ((k ^ first[0]) >> 1)
            copies.append(
                pltpu.make_async_copy(
                    done.at[step],
                    out.at[pl.ds(pl.multiple_of(to * chunk, chunk), chunk), :],
                    sems.at[step],
                )
            )
            copies[-1].start()
    for copy in copies:
        copy.wait()


def swap(array, even, odd=None):
    masks = (even, even if odd is None else odd)
    peers = lax.axis_size("depth")
    pairs = [(2 * d + c, 2 * (d ^ masks[c]) + c) for d in range(peers) for c in range(2)]
    return lax.ppermute(array, AXES, pairs)


def swap_cores(array):
    return lax.ppermute(array, "samp", [(0, 1), (1, 0)])


def staged(n, act, halves, odd, weights, states, width, count):
    chans = act.shape[1]
    rows = 27 * chans
    pieces = n * n
    size = rows // (2 * pieces)
    wide = -(-size // 16) * 16
    step = 2 * size - wide
    depth = lax.axis_index("depth")
    one = lambda value: jnp.reshape(value, (1,)).astype(jnp.int32)
    core, first, second = one(lax.axis_index("samp")), one(depth % n), one(depth // n)
    f32 = lambda *shape: jax.ShapeDtypeStruct(shape, jnp.float32)
    b16 = lambda *shape: jax.ShapeDtypeStruct(shape, jnp.bfloat16)
    shift = pltpu.VMEM((3, act.shape[0] + 2 * width, 3 * chans), jnp.bfloat16)
    flops = 2 * rows * chans * act.shape[0]
    third = 9 * chans
    low, high = -(-third // (2 * size)), 2 * third // (2 * size)
    early, late = high - low, pieces - high + low
    edges, kept, sent = call(
        functools.partial(early_body, width, 2 * size, low, step),
        (f32(third - 2 * size * early, chans),) + (f32(early, wide, chans),) * 2,
        3,
        flops=flops // 3,
        scratch=[shift, pltpu.VMEM((third, chans), jnp.float32)],
        limit=6 << 20,
    )(core, act, *halves[:2])
    came = swap_cores(sent)
    keep, sent = call(
        functools.partial(late_body, width, 2 * size, low, step),
        (f32(late, wide, chans),) * 2,
        7,
        flops=flops,
        scratch=[shift, pltpu.VMEM((rows, chans), jnp.float32)],
        limit=6 << 20,
        scalars=2,
    )(core, odd, act, *halves[2:], edges, came)
    come = swap_cores(sent)
    parts = call(
        functools.partial(merge_body, n, 0, low), (f32(n, wide, chans),) * n, 4, scalars=3
    )(core, first, second, keep, come, kept, came)
    got = [parts[0]] + [swap(parts[m], m, m * n) for m in range(1, n)]
    grad_input, token = call(
        functools.partial(input_body, width),
        (b16(*act.shape), f32(8, chans)),
        7,
        flops=flops,
        moved=4 << 20,
        scratch=[shift],
        limit=6 << 20,
    )(odd, weights, *halves)
    parts = call(
        functools.partial(merge_body, n, 1, None),
        (f32(1, wide, chans),) * n,
        n + 1,
        scalars=3,
    )(core, first, second, *got, token)
    got = [parts[0]] + [swap(parts[m], m * n, m) for m in range(1, n)]
    states = [s.reshape(size, chans) for s in states]
    share = call(functools.partial(share_body, count), b16(1, wide, chans), n + 3)(
        core, *got, *states
    )
    *fresh, token = call(
        functools.partial(adam_body, count),
        (f32(size, chans),) * 4 + (f32(8, chans),),
        n + 4,
    )(core, *got, *states, share)
    got = [share] + [swap(share, m * n) for m in range(1, n)]
    line = call(gather_body, b16(n, wide, chans), n + 1)(core, *got, token)
    own = [line] + [swap(line, m) for m in range(1, n)]
    peer = [swap_cores(block) for block in own]
    chunks = pieces // 2
    new_weights = call(
        functools.partial(place_body, n, size),
        b16(rows, chans),
        2 * n,
        scratch=[
            pltpu.VMEM((4 * size, chans), jnp.float32),
            pltpu.VMEM((chunks, 4 * size, chans), jnp.bfloat16),
            pltpu.SemaphoreType.DMA((chunks,)),
        ],
        scalars=3,
        spec=pl.BlockSpec(memory_space=pltpu.HBM),
    )(core, first, second, *own, *peer)
    return grad_input, [x.reshape(-1) for x in fresh], new_weights


def plain(act, halves, odd, weights, states, width, count):
    chans = act.shape[1]
    rows = 27 * chans
    shift = pltpu.VMEM((3, act.shape[0] + 2 * width, 3 * chans), jnp.bfloat16)
    grads = call(
        functools.partial(all_filter_body, width),
        jax.ShapeDtypeStruct((rows, chans), jnp.float32),
        7,
        scratch=[shift],
        limit=6 << 20,
    )(odd, act, *halves)
    grad_input, _ = call(
        functools.partial(input_body, width),
        (
            jax.ShapeDtypeStruct(act.shape, jnp.bfloat16),
            jax.ShapeDtypeStruct((8, chans), jnp.float32),
        ),
        7,
        scratch=[shift],
        limit=6 << 20,
    )(odd, weights, *halves)
    total = lax.psum_scatter(grads.reshape(-1), AXES, scatter_dimension=0, tiled=True)
    master, moment, second = states
    grad = total * jnp.float32(1.0 / count**0.5)
    new_moment = 0.9 * moment + 0.1 * grad
    new_second = 0.999 * second + 0.001 * grad * grad
    new_master = master - 0.01 * (new_moment / first_fix) / (
        jnp.sqrt(new_second / second_fix) + 1e-08
    )
    whole = lax.all_gather(new_master.astype(jnp.bfloat16), AXES, axis=0, tiled=True)
    return grad_input, [grad, new_moment, new_second, new_master], whole


def neighbours(top, bottom):
    peers = lax.axis_size("depth")
    move = lambda array, pairs: lax.ppermute(array, "depth", pairs)
    partner = [(i, i ^ 1) for i in range(peers)]
    direct = [(i - 1, i) for i in range(2, peers, 2)] + [(i + 1, i) for i in range(1, peers - 1, 2)]
    relayed = [(i - 2, i) for i in range(2, peers, 2)] + [(i + 2, i) for i in range(1, peers - 1, 2)]
    partner_top = move(top, partner)
    partner_bottom = move(bottom, partner)
    other_bottom = move(bottom, direct)
    other_top = move(partner_top, relayed)
    return (top, bottom, partner_top, partner_bottom, other_top, other_bottom)


def local(n, activations, preact, out_grad, weights, master, moment, second):
    samples, planes, height, width, chans = activations.shape
    count = samples * lax.axis_size("samp") * planes * lax.axis_size("depth") * height * width
    act = activations.reshape(-1, chans)
    half = act.shape[0] // 2

    def cotangent(part):
        slope = jnp.where(preact.reshape(-1, chans)[part] > 0, jnp.float32(1.0), jnp.float32(0.01))
        return (out_grad.reshape(-1, chans)[part].astype(jnp.float32) * slope).astype(jnp.bfloat16)

    halves = neighbours(cotangent(slice(0, half)), cotangent(slice(half, None)))
    odd = jnp.reshape(lax.axis_index("depth") % 2, (1,)).astype(jnp.int32)
    taps = weights.reshape(27, chans, chans)
    states = (master, moment, second)
    if n:
        result = staged(n, act, halves, odd, taps, states, width, count)
    else:
        result = plain(act, halves, odd, taps, states, width, count)
    grad_input, fresh, whole = result
    return (grad_input.reshape(activations.shape), *fresh, whole.reshape(weights.shape))


def stages(mesh):
    n = math.isqrt(mesh.shape["depth"])
    ready = mesh.shape["samp"] == 2 and n * n == mesh.shape["depth"] and n & (n - 1) == 0
    return n if ready else 0


def solution(mesh):
    split = P("samp", "depth", None, None, None)
    shard = P(AXES)
    n = stages(mesh)

    def body(*args):
        return local(n, *args)

    return jax.shard_map(
        body,
        mesh=mesh,
        in_specs=(split, split, split, P(), shard, shard, shard),
        out_specs=(split, shard, shard, shard, shard, P()),
        check_vma=False,
    )
```

```python
import functools
import math
import jax
import jax.numpy as jnp
from jax import lax
from jax.experimental import pallas as pl
from jax.experimental.pallas import tpu as pltpu
from jax.sharding import PartitionSpec as P

first_fix = 1.0
second_fix = 0.63230457524
AXES = ("depth", "samp")
ORDERS = {
    "first": ((2, 1, 3), (2, 1, 3)),
    "second": ((3, 2, 1), (3, 1, 2)),
    "line": ((3, 2, 1), (3, 2, 1)),
    "plane": ((3, 2, 1), (3, 2, 1)),
}
VMEM = pl.BlockSpec(memory_space=pltpu.VMEM)
SMEM = pl.BlockSpec(memory_space=pltpu.SMEM)
HBM = pl.BlockSpec(memory_space=pltpu.HBM)


def masks_of(stage, n):
    plain = (tuple(range(n - 1, 0, -1)),) * 2
    orders = ORDERS[stage] if n == 4 else plain
    return ((0, 0), *list(zip(*orders))[::-1])


def exchange(stage, n, terms, scales):
    got = [terms[0]]
    for t, masks in enumerate(masks_of(stage, n)):
        if t > 0:
            got.append(swap(terms[t], *(m * scale for m, scale in zip(masks, scales))))
    return got


def call(body, outs, n_in, flops=0, moved=0, scratch=(), limit=2 << 20, scalars=1):
    return pl.pallas_call(
        body,
        out_shape=outs,
        in_specs=[SMEM] * scalars + [VMEM] * n_in,
        out_specs=jax.tree.map(lambda _: VMEM, outs),
        scratch_shapes=list(scratch),
        cost_estimate=pl.CostEstimate(flops=flops, bytes_accessed=moved, transcendentals=0),
        compiler_params=pltpu.CompilerParams(vmem_limit_bytes=limit),
    )


def fill_shifted(shifted, slot, halves, width):
    plane = jnp.concatenate([half[...] for half in halves], axis=0)
    rows, chans = plane.shape
    wide = plane.astype(jnp.float32)
    column = lax.broadcasted_iota(jnp.int32, (rows, chans), 0) % width
    nxt = jnp.where(column == width - 1, 0.0, pltpu.roll(wide, rows - 1, 0))
    prv = jnp.where(column == 0, 0.0, pltpu.roll(wide, 1, 0))
    edge = jnp.zeros((width, 3 * chans), plane.dtype)
    shifted[slot, 0:width, :] = edge
    shifted[slot, width + rows : 2 * width + rows, :] = edge
    body = slice(width, width + rows)
    shifted[slot, body, 0:chans] = nxt.astype(plane.dtype)
    shifted[slot, body, chans : 2 * chans] = plane
    shifted[slot, body, 2 * chans :] = prv.astype(plane.dtype)


def planes_of(odd, refs):
    yield 0, 1, refs[0:2]
    yield 1, 2 * odd, refs[2:4]
    yield 2, 2 - 2 * odd, refs[4:6]


def filter_taps(width, act, planes, grads, shifted):
    left = act[...]
    rows, chans = left.shape
    for slot, deep, plane in planes:
        fill_shifted(shifted, slot, plane, width)
        for b in range(3):
            part = shifted[slot, (2 - b) * width : (2 - b) * width + rows, :]
            out = lax.dot_general(
                left, part, (((0,), (0,)), ((), ())), preferred_element_type=jnp.float32
            )
            for c in range(3):
                at = ((deep * 3 + b) * 3 + c) * chans
                if not isinstance(at, int):
                    at = pl.multiple_of(at, chans)
                grads[pl.ds(at, chans), :] = out[:, c * chans : (c + 1) * chans]


def pick(source, keep, send, core, step, starts):
    wide = keep.shape[1]
    for at, slot in starts:
        keep[slot] = source[pl.ds(pl.multiple_of(at + core * step, 8), wide), :]
        send[slot] = source[pl.ds(pl.multiple_of(at + (1 - core) * step, 8), wide), :]


def early_body(width, chip, step, core, act, top, bottom, edges, keep, send, shifted, grads):
    filter_taps(width, act, [(0, 0, (top, bottom))], grads, shifted)
    lead, count = edges.shape[0] // 2, keep.shape[0]
    pick(grads, keep, send, core[0], step, [(lead + k * chip, k) for k in range(count)])
    edges[0:lead, :] = grads[0:lead, :]
    edges[lead:, :] = grads[lead + count * chip :, :]


def outer_taps(width, chip, side, last, act, halves, grads, shifted):
    filter_taps(width, act, [(0, 0, halves)], grads, shifted)
    edge = grads.shape[0] - side * chip
    return last * edge, pl.multiple_of((1 - last) * side * chip, 8), edge


def near_body(width, chip, step, core, odd, act, top, bottom, rim, keep, send, shifted, grads):
    side = keep.shape[0]
    start, at, edge = outer_taps(width, chip, side, odd[0], act, (top, bottom), grads, shifted)
    pick(grads, keep, send, core[0], step, [(start + k * chip, k) for k in range(side)])
    rim[...] = grads[pl.ds(at, edge), :]


def late_body(width, chip, step, core, odd, act, top, bottom, edges, rim, keep, send, *scratch):
    shifted, grads, ends = scratch
    side = keep.shape[0] - 2
    last = 1 - odd[0]
    start, at, edge = outer_taps(width, chip, side, last, act, (top, bottom), grads, shifted)
    pick(grads, keep, send, core[0], step, [(start + k * chip, k) for k in range(side)])
    lead = chip - edge
    ends[edge:chip, :] = edges[0:lead, :]
    ends[chip : chip + lead, :] = edges[lead:, :]
    ends[pl.ds(pl.multiple_of(last * (chip + lead), 8), edge), :] = grads[pl.ds(at, edge), :]
    ends[pl.ds(pl.multiple_of((1 - last) * (chip + lead), 8), edge), :] = rim[...]
    pick(ends, keep, send, core[0], step, [(0, side), (chip, side + 1)])


def all_filter_body(width, odd, act, *refs):
    halves, (grads, shifted) = refs[:6], refs[6:]
    filter_taps(width, act, planes_of(odd[0], halves), grads, shifted)


def input_body(width, odd, weights, *refs):
    halves, (out, token, shifted) = refs[:6], refs[6:]
    rows, chans = out.shape
    total = jnp.zeros((rows, chans), jnp.float32)
    for slot, deep, plane in planes_of(odd[0], halves):
        fill_shifted(shifted, slot, plane, width)
        for b in range(3):
            part = shifted[slot, (2 - b) * width : (2 - b) * width + rows, :]
            taps = [weights[(deep * 3 + b) * 3 + c] for c in range(3)]
            total = total + lax.dot_general(
                part,
                jnp.concatenate(taps, axis=1),
                (((1,), (1,)), ((), ())),
                preferred_element_type=jnp.float32,
            )
    out[...] = total.astype(out.dtype)
    token[...] = jnp.zeros(token.shape, token.dtype)


def merge_body(n, stage, swapped, split, core, first, second, *refs):
    outs = refs[len(refs) - n :]
    terms = [r for r in refs[: len(refs) - n] if len(r.shape) == 3]
    flip = core[0] != swapped
    own = jnp.where(flip, second[0], first[0])
    group, other = jnp.where(flip, n, 1), jnp.where(flip, 1, n)
    for j, masks in enumerate(masks_of(stage, n)):
        at = own ^ jnp.where(core[0] == 0, *masks)
        for h in range(outs[j].shape[0]):
            piece = at * group + h * other if outs[j].shape[0] > 1 else at
            if not split:
                outs[j][h] = functools.reduce(lambda x, y: x + y, [term[piece] for term in terms])
                continue
            side, count = terms[2].shape[0], terms[4].shape[0]
            low, high = side + 1, side + 1 + count
            inner = (piece >= low) & (piece < high)
            upper = (piece > high).astype(jnp.int32)
            outer = jnp.clip(piece - upper * (high + 1), 0, side - 1)
            across = (piece == side) | (piece == high)
            near = (upper == (first[0] & 1)) & jnp.logical_not(across | inner)
            late = jnp.where(across, side + (piece == high).astype(jnp.int32), outer)
            early = jnp.clip(piece - low, 0, count - 1)
            rest = jnp.logical_not(inner | near)
            for chosen, pair, index in ((inner, 4, early), (near, 2, outer), (rest, 0, late)):

                @pl.when(chosen)
                def _(out=outs[j], pair=pair, index=index, h=h):
                    out[h] = terms[pair][index] + terms[pair + 1][index]


def adam_step(count, core, terms, master, moment, second):
    total = terms[0][0]
    for term in terms[1:]:
        total = total + term[0]
    size = master.shape[0]
    skip = total.shape[0] - size
    raw = jnp.where(core == 0, total[0:size], total[skip : skip + size])
    grad = raw * jnp.float32(1.0 / count**0.5)
    new_moment = 0.9 * moment[...] + 0.1 * grad
    new_second = 0.999 * second[...] + 0.001 * grad * grad
    new_master = master[...] - 0.01 * (new_moment / first_fix) / (
        jnp.sqrt(new_second / second_fix) + 1e-08
    )
    return grad, new_moment, new_second, new_master


def share_body(count, core, *refs):
    terms, (master, moment, second, share) = refs[:-4], refs[-4:]
    size, chans = master.shape
    new_master = adam_step(count, core[0], terms, master, moment, second)[3]
    share[0, 0:size, :] = new_master.astype(share.dtype)
    share[0, size:, :] = jnp.zeros((share.shape[1] - size, chans), share.dtype)


def adam_body(count, core, *refs):
    terms, (master, moment, second, _), outs = refs[:-9], refs[-9:-5], refs[-5:]
    for out, value in zip(outs, adam_step(count, core[0], terms, master, moment, second)):
        out[...] = value
    outs[4][...] = jnp.zeros(outs[4].shape, outs[4].dtype)


def gather_body(me, *refs):
    blocks = [r for r in refs[:-1] if len(r.shape) == 3]
    for k, ref in enumerate(blocks):
        refs[-1][k] = ref[0]


def place_body(n, size, groups, core, first, second, *refs):
    count = len(groups)
    own, peer, (out, done, sems) = refs[:count], refs[count : 2 * count], refs[-3:]
    copies = []
    for step in range(count * n):
        z, mask = step // count, groups[step % count]
        piece = (z ^ second[0]) * n + (mask ^ first[0])
        rows = pl.ds(pl.multiple_of(piece * 2 * size, 2 * size), 2 * size)
        copies.append(pltpu.make_async_copy(done.at[step], out.at[rows, :], sems.at[step]))

    def find(stage, c, mask):
        return [masks[c] for masks in masks_of(stage, n)].index(mask)

    def write(other):
        for step in range(count * n):
            z, group = divmod(step, count)
            for c in range(2):
                block = (own, peer)[c ^ other][group][find("line", c, z)]
                done[step, c * size : (c + 1) * size, :] = block[0:size]
            copies[step].start()

    for other in range(2):
        pl.when(core[0] == other)(functools.partial(write, other))
    for copy in copies:
        copy.wait()


def place(n, size, rows, groups, scalars, own, peer, earlier):
    chans = own[0].shape[2]
    steps = len(groups) * n
    return pl.pallas_call(
        functools.partial(place_body, n, size, groups),
        out_shape=jax.ShapeDtypeStruct((rows, chans), jnp.bfloat16),
        in_specs=[SMEM] * 3 + [VMEM] * (2 * len(groups)) + [HBM] * len(earlier),
        out_specs=HBM,
        scratch_shapes=[
            pltpu.VMEM((steps, 2 * size, chans), jnp.bfloat16),
            pltpu.SemaphoreType.DMA((steps,)),
        ],
        input_output_aliases={3 + 2 * len(groups): 0} if earlier else {},
        cost_estimate=pl.CostEstimate(flops=0, bytes_accessed=0, transcendentals=0),
        compiler_params=pltpu.CompilerParams(vmem_limit_bytes=2 << 20),
    )(*scalars, *own, *peer, *earlier)


def swap(array, *masks):
    peers = lax.axis_size("depth")
    pairs = [(2 * d + c, 2 * (d ^ masks[c]) + c) for d in range(peers) for c in range(2)]
    return lax.ppermute(array, AXES, pairs)


def swap_cores(array):
    return lax.ppermute(array, "samp", [(0, 1), (1, 0)])


def staged(n, act, halves, odd, weights, states, width, count):
    chans = act.shape[1]
    rows = 27 * chans
    pieces = n * n
    size = rows // (2 * pieces)
    wide = -(-size // 16) * 16
    step = 2 * size - wide
    depth = lax.axis_index("depth")
    one = lambda value: jnp.reshape(value, (1,)).astype(jnp.int32)
    core, first, second = one(lax.axis_index("samp")), one(depth % n), one(depth // n)
    f32 = lambda *shape: jax.ShapeDtypeStruct(shape, jnp.float32)
    b16 = lambda *shape: jax.ShapeDtypeStruct(shape, jnp.bfloat16)
    shift = pltpu.VMEM((1, act.shape[0] + 2 * width, 3 * chans), jnp.bfloat16)
    shifts = pltpu.VMEM((3, act.shape[0] + 2 * width, 3 * chans), jnp.bfloat16)
    flops = 2 * rows * chans * act.shape[0]
    third, chip = 9 * chans, 2 * size
    side = third // chip
    inner = pieces - 2 * side - 2
    edge = third - side * chip
    grads = pltpu.VMEM((third, chans), jnp.float32)
    filters = functools.partial(call, flops=flops // 3, limit=6 << 20)
    half = lambda count: (f32(count, wide, chans),) * 2
    edges, early, sent = filters(
        functools.partial(early_body, width, chip, step),
        (f32(2 * (chip - edge), chans), *half(inner)),
        3,
        scratch=[shift, grads],
    )(core, act, *halves[:2])
    early_come = swap_cores(sent)
    rim, near, sent = filters(
        functools.partial(near_body, width, chip, step),
        (f32(edge, chans), *half(side)),
        3,
        scratch=[shift, grads],
        scalars=2,
    )(core, odd, act, *halves[2:4])
    near_come = swap_cores(sent)
    late, sent = filters(
        functools.partial(late_body, width, chip, step),
        half(side + 2),
        5,
        scratch=[shift, grads, pltpu.VMEM((2 * chip, chans), jnp.float32)],
        scalars=2,
    )(core, odd, act, *halves[4:], edges, rim)
    late_come = swap_cores(sent)
    terms = (late, late_come, near, near_come, early, early_come)
    parts = call(
        functools.partial(merge_body, n, "first", 0, True), (f32(n, wide, chans),) * n, 6, scalars=3
    )(core, first, second, *terms)
    got = exchange("first", n, parts, (1, n))
    grad_input, token = call(
        functools.partial(input_body, width),
        (b16(*act.shape), f32(8, chans)),
        7,
        flops=flops,
        moved=4 << 20,
        scratch=[shifts],
        limit=6 << 20,
    )(odd, weights, *halves)
    parts = call(
        functools.partial(merge_body, n, "second", 1, False),
        (f32(1, wide, chans),) * n,
        n + 1,
        scalars=3,
    )(core, first, second, *got, token)
    got = exchange("second", n, parts, (n, 1))
    states = [s.reshape(size, chans) for s in states]
    share = call(functools.partial(share_body, count), b16(1, wide, chans), n + 3)(
        core, *got, *states
    )
    *fresh, token = call(
        functools.partial(adam_body, count),
        (f32(size, chans),) * 4 + (f32(8, chans),),
        n + 4,
    )(core, *got, *states, share)
    got = exchange("line", n, [share] * n, (n, n))
    line = call(gather_body, b16(n, wide, chans), n + 1)(core, *got, token)
    own = exchange("plane", n, [line] * n, (1, 1))
    peer = []
    for block in own:
        peer.append(swap_cores(block))
    new_weights, where = [], [list(zip(*masks_of("plane", n)))[c] for c in range(2)]
    assert where[0] == where[1]
    at = (core, first, second)
    for chosen in ((0, n - 1), tuple(range(1, n - 1))):
        groups = tuple(where[0][t] for t in chosen)
        mine, theirs = [own[t] for t in chosen], [peer[t] for t in chosen]
        new_weights = [place(n, size, rows, groups, at, mine, theirs, new_weights)]
    new_weights = new_weights[0]
    return grad_input, [x.reshape(-1) for x in fresh], new_weights


def plain(act, halves, odd, weights, states, width, count):
    chans = act.shape[1]
    rows = 27 * chans
    shift = pltpu.VMEM((3, act.shape[0] + 2 * width, 3 * chans), jnp.bfloat16)
    grads = call(
        functools.partial(all_filter_body, width),
        jax.ShapeDtypeStruct((rows, chans), jnp.float32),
        7,
        scratch=[shift],
        limit=6 << 20,
    )(odd, act, *halves)
    grad_input, _ = call(
        functools.partial(input_body, width),
        (
            jax.ShapeDtypeStruct(act.shape, jnp.bfloat16),
            jax.ShapeDtypeStruct((8, chans), jnp.float32),
        ),
        7,
        scratch=[shift],
        limit=6 << 20,
    )(odd, weights, *halves)
    total = lax.psum_scatter(grads.reshape(-1), AXES, scatter_dimension=0, tiled=True)
    master, moment, second = states
    grad = total * jnp.float32(1.0 / count**0.5)
    new_moment = 0.9 * moment + 0.1 * grad
    new_second = 0.999 * second + 0.001 * grad * grad
    new_master = master - 0.01 * (new_moment / first_fix) / (
        jnp.sqrt(new_second / second_fix) + 1e-08
    )
    whole = lax.all_gather(new_master.astype(jnp.bfloat16), AXES, axis=0, tiled=True)
    return grad_input, [grad, new_moment, new_second, new_master], whole


def neighbours(top, bottom):
    peers = lax.axis_size("depth")
    move = lambda array, pairs: lax.ppermute(array, "depth", pairs)
    partner = [(i, i ^ 1) for i in range(peers)]
    direct = [(i - 1, i) for i in range(2, peers, 2)] + [(i + 1, i) for i in range(1, peers - 1, 2)]
    relayed = [(i - 2, i) for i in range(2, peers, 2)] + [(i + 2, i) for i in range(1, peers - 1, 2)]
    partner_top = move(top, partner)
    partner_bottom = move(bottom, partner)
    other_bottom = move(bottom, direct)
    other_top = move(partner_top, relayed)
    return (top, bottom, partner_top, partner_bottom, other_top, other_bottom)


def local(n, activations, preact, out_grad, weights, master, moment, second):
    samples, planes, height, width, chans = activations.shape
    count = samples * lax.axis_size("samp") * planes * lax.axis_size("depth") * height * width
    act = activations.reshape(-1, chans)
    half = act.shape[0] // 2

    def cotangent(part):
        slope = jnp.where(preact.reshape(-1, chans)[part] > 0, jnp.float32(1.0), jnp.float32(0.01))
        return (out_grad.reshape(-1, chans)[part].astype(jnp.float32) * slope).astype(jnp.bfloat16)

    halves = neighbours(cotangent(slice(0, half)), cotangent(slice(half, None)))
    odd = jnp.reshape(lax.axis_index("depth") % 2, (1,)).astype(jnp.int32)
    taps = weights.reshape(27, chans, chans)
    states = (master, moment, second)
    if n:
        result = staged(n, act, halves, odd, taps, states, width, count)
    else:
        result = plain(act, halves, odd, taps, states, width, count)
    grad_input, fresh, whole = result
    return (grad_input.reshape(activations.shape), *fresh, whole.reshape(weights.shape))


def stages(mesh):
    n = math.isqrt(mesh.shape["depth"])
    ready = mesh.shape["samp"] == 2 and n * n == mesh.shape["depth"] and n & (n - 1) == 0
    return n if ready else 0


def solution(mesh):
    split = P("samp", "depth", None, None, None)
    shard = P(AXES)
    n = stages(mesh)

    def body(*args):
        return local(n, *args)

    return jax.shard_map(
        body,
        mesh=mesh,
        in_specs=(split, split, split, P(), shard, shard, shard),
        out_specs=(split, shard, shard, shard, shard, P()),
        check_vma=False,
    )
```

```python
import functools
import math
import jax
import jax.numpy as jnp
from jax import lax
from jax.experimental import pallas as pl
from jax.experimental.pallas import tpu as pltpu
from jax.sharding import PartitionSpec as P

first_fix = 1.0
second_fix = 0.63230457524
AXES = ("depth", "samp")
ORDERS = {
    "first": ((2, 1, 3), (2, 1, 3)),
    "second": ((3, 2, 1), (3, 1, 2)),
    "line": ((3, 2, 1), (3, 2, 1)),
    "plane": ((3, 2, 1), (3, 2, 1)),
}
VMEM = pl.BlockSpec(memory_space=pltpu.VMEM)
SMEM = pl.BlockSpec(memory_space=pltpu.SMEM)
HBM = pl.BlockSpec(memory_space=pltpu.HBM)


def masks_of(stage, n):
    plain = (tuple(range(n - 1, 0, -1)),) * 2
    orders = ORDERS[stage] if n == 4 else plain
    return ((0, 0), *list(zip(*orders))[::-1])


def exchange(stage, n, terms, scales):
    got = [terms[0]]
    for t, masks in enumerate(masks_of(stage, n)):
        if t > 0:
            got.append(swap(terms[t], *(m * scale for m, scale in zip(masks, scales))))
    return got


def call(body, outs, n_in, flops=0, moved=0, scratch=(), limit=2 << 20, scalars=1):
    return pl.pallas_call(
        body,
        out_shape=outs,
        in_specs=[SMEM] * scalars + [VMEM] * n_in,
        out_specs=jax.tree.map(lambda _: VMEM, outs),
        scratch_shapes=list(scratch),
        cost_estimate=pl.CostEstimate(flops=flops, bytes_accessed=moved, transcendentals=0),
        compiler_params=pltpu.CompilerParams(vmem_limit_bytes=limit),
    )


def fill_shifted(shifted, slot, halves, width):
    plane = jnp.concatenate([half[...] for half in halves], axis=0)
    rows, chans = plane.shape
    wide = plane.astype(jnp.float32)
    column = lax.broadcasted_iota(jnp.int32, (rows, chans), 0) % width
    nxt = jnp.where(column == width - 1, 0.0, pltpu.roll(wide, rows - 1, 0))
    prv = jnp.where(column == 0, 0.0, pltpu.roll(wide, 1, 0))
    edge = jnp.zeros((width, 3 * chans), plane.dtype)
    shifted[slot, 0:width, :] = edge
    shifted[slot, width + rows : 2 * width + rows, :] = edge
    body = slice(width, width + rows)
    shifted[slot, body, 0:chans] = nxt.astype(plane.dtype)
    shifted[slot, body, chans : 2 * chans] = plane
    shifted[slot, body, 2 * chans :] = prv.astype(plane.dtype)


def planes_of(odd, refs):
    yield 0, 1, refs[0:2]
    yield 1, 2 * odd, refs[2:4]
    yield 2, 2 - 2 * odd, refs[4:6]


def filter_taps(width, act, planes, grads, shifted):
    left = act[...]
    rows, chans = left.shape
    for slot, deep, plane in planes:
        fill_shifted(shifted, slot, plane, width)
        for b in range(3):
            part = shifted[slot, (2 - b) * width : (2 - b) * width + rows, :]
            out = lax.dot_general(
                left, part, (((0,), (0,)), ((), ())), preferred_element_type=jnp.float32
            )
            for c in range(3):
                at = ((deep * 3 + b) * 3 + c) * chans
                if not isinstance(at, int):
                    at = pl.multiple_of(at, chans)
                grads[pl.ds(at, chans), :] = out[:, c * chans : (c + 1) * chans]


def pick(source, keep, send, core, step, starts):
    wide = keep.shape[1]
    for at, slot in starts:
        keep[slot] = source[pl.ds(pl.multiple_of(at + core * step, 8), wide), :]
        send[slot] = source[pl.ds(pl.multiple_of(at + (1 - core) * step, 8), wide), :]


def early_body(width, chip, step, core, act, top, bottom, edges, keep, send, shifted, grads):
    filter_taps(width, act, [(0, 0, (top, bottom))], grads, shifted)
    lead, count = edges.shape[0] // 2, keep.shape[0]
    pick(grads, keep, send, core[0], step, [(lead + k * chip, k) for k in range(count)])
    edges[0:lead, :] = grads[0:lead, :]
    edges[lead:, :] = grads[lead + count * chip :, :]


def outer_taps(width, chip, side, last, act, halves, grads, shifted):
    filter_taps(width, act, [(0, 0, halves)], grads, shifted)
    edge = grads.shape[0] - side * chip
    return last * edge, pl.multiple_of((1 - last) * side * chip, 8), edge


def near_body(width, chip, step, core, odd, act, top, bottom, rim, keep, send, shifted, grads):
    side = keep.shape[0]
    start, at, edge = outer_taps(width, chip, side, odd[0], act, (top, bottom), grads, shifted)
    pick(grads, keep, send, core[0], step, [(start + k * chip, k) for k in range(side)])
    rim[...] = grads[pl.ds(at, edge), :]


def late_body(width, chip, step, core, odd, act, top, bottom, edges, rim, keep, send, *scratch):
    shifted, grads, ends = scratch
    side = keep.shape[0] - 2
    last = 1 - odd[0]
    start, at, edge = outer_taps(width, chip, side, last, act, (top, bottom), grads, shifted)
    pick(grads, keep, send, core[0], step, [(start + k * chip, k) for k in range(side)])
    lead = chip - edge
    ends[edge:chip, :] = edges[0:lead, :]
    ends[chip : chip + lead, :] = edges[lead:, :]
    ends[pl.ds(pl.multiple_of(last * (chip + lead), 8), edge), :] = grads[pl.ds(at, edge), :]
    ends[pl.ds(pl.multiple_of((1 - last) * (chip + lead), 8), edge), :] = rim[...]
    pick(ends, keep, send, core[0], step, [(0, side), (chip, side + 1)])


def all_filter_body(width, odd, act, *refs):
    halves, (grads, shifted) = refs[:6], refs[6:]
    filter_taps(width, act, planes_of(odd[0], halves), grads, shifted)


def input_body(width, odd, weights, *refs):
    halves, (out, token, shifted) = refs[:6], refs[6:]
    rows, chans = out.shape
    total = jnp.zeros((rows, chans), jnp.float32)
    for slot, deep, plane in planes_of(odd[0], halves):
        fill_shifted(shifted, slot, plane, width)
        for b in range(3):
            part = shifted[slot, (2 - b) * width : (2 - b) * width + rows, :]
            taps = [weights[(deep * 3 + b) * 3 + c] for c in range(3)]
            total = total + lax.dot_general(
                part,
                jnp.concatenate(taps, axis=1),
                (((1,), (1,)), ((), ())),
                preferred_element_type=jnp.float32,
            )
    out[...] = total.astype(out.dtype)
    token[...] = jnp.zeros(token.shape, token.dtype)


def add_split(odd, terms, sums):
    side, count = terms[2].shape[0], terms[4].shape[0]
    low, high = side + 1, side + 1 + count
    for piece in range(sums.shape[0]):
        if low <= piece < high:
            pair, index = 4, piece - low
        elif piece in (side, high):
            pair, index = 0, side + (piece == high)
        else:
            upper = piece > high
            pair, index = (2 if upper == odd else 0), piece - upper * (high + 1)
        sums[piece] = terms[pair][index] + terms[pair + 1][index]


def merge_body(n, stage, swapped, split, core, first, second, *refs):
    end = len(refs) - split
    outs = refs[end - n : end]
    terms = [r for r in refs[: end - n] if len(r.shape) == 3]
    if split:
        for odd in range(2):
            pl.when((first[0] & 1) == odd)(functools.partial(add_split, odd, terms, refs[-1]))
        terms = [refs[-1]]
    flip = core[0] != swapped
    own = jnp.where(flip, second[0], first[0])
    group, other = jnp.where(flip, n, 1), jnp.where(flip, 1, n)
    for j, masks in enumerate(masks_of(stage, n)):
        at = own ^ jnp.where(core[0] == 0, *masks)
        for h in range(outs[j].shape[0]):
            piece = at * group + h * other if outs[j].shape[0] > 1 else at
            outs[j][h] = functools.reduce(lambda x, y: x + y, [term[piece] for term in terms])


def adam_step(count, core, terms, master, moment, second):
    total = terms[0][0]
    for term in terms[1:]:
        total = total + term[0]
    size = master.shape[0]
    skip = total.shape[0] - size
    raw = jnp.where(core == 0, total[0:size], total[skip : skip + size])
    grad = raw * jnp.float32(1.0 / count**0.5)
    new_moment = 0.9 * moment[...] + 0.1 * grad
    new_second = 0.999 * second[...] + 0.001 * grad * grad
    new_master = master[...] - 0.01 * (new_moment / first_fix) / (
        jnp.sqrt(new_second / second_fix) + 1e-08
    )
    return grad, new_moment, new_second, new_master


def share_body(count, core, *refs):
    terms, (master, moment, second, share) = refs[:-4], refs[-4:]
    size, chans = master.shape
    new_master = adam_step(count, core[0], terms, master, moment, second)[3]
    share[0, 0:size, :] = new_master.astype(share.dtype)
    share[0, size:, :] = jnp.zeros((share.shape[1] - size, chans), share.dtype)


def adam_body(count, core, *refs):
    terms, (master, moment, second, _), outs = refs[:-9], refs[-9:-5], refs[-5:]
    for out, value in zip(outs, adam_step(count, core[0], terms, master, moment, second)):
        out[...] = value
    outs[4][...] = jnp.zeros(outs[4].shape, outs[4].dtype)


def gather_body(me, *refs):
    blocks = [r for r in refs[:-1] if len(r.shape) == 3]
    for k, ref in enumerate(blocks):
        refs[-1][k] = ref[0]


def place_body(n, size, groups, core, first, second, *refs):
    count = len(groups)
    own, peer, (out, done, sems) = refs[:count], refs[count : 2 * count], refs[-3:]
    copies = []
    for step in range(count * n):
        z, mask = step // count, groups[step % count]
        piece = (z ^ second[0]) * n + (mask ^ first[0])
        rows = pl.ds(pl.multiple_of(piece * 2 * size, 2 * size), 2 * size)
        copies.append(pltpu.make_async_copy(done.at[step], out.at[rows, :], sems.at[step]))

    def find(stage, c, mask):
        return [masks[c] for masks in masks_of(stage, n)].index(mask)

    def write(other):
        for step in range(count * n):
            z, group = divmod(step, count)
            for c in range(2):
                block = (own, peer)[c ^ other][group][find("line", c, z)]
                done[step, c * size : (c + 1) * size, :] = block[0:size]
            copies[step].start()

    for other in range(2):
        pl.when(core[0] == other)(functools.partial(write, other))
    for copy in copies:
        copy.wait()


def place(n, size, rows, groups, scalars, own, peer, earlier):
    chans = own[0].shape[2]
    steps = len(groups) * n
    return pl.pallas_call(
        functools.partial(place_body, n, size, groups),
        out_shape=jax.ShapeDtypeStruct((rows, chans), jnp.bfloat16),
        in_specs=[SMEM] * 3 + [VMEM] * (2 * len(groups)) + [HBM] * len(earlier),
        out_specs=HBM,
        scratch_shapes=[
            pltpu.VMEM((steps, 2 * size, chans), jnp.bfloat16),
            pltpu.SemaphoreType.DMA((steps,)),
        ],
        input_output_aliases={3 + 2 * len(groups): 0} if earlier else {},
        cost_estimate=pl.CostEstimate(flops=0, bytes_accessed=0, transcendentals=0),
        compiler_params=pltpu.CompilerParams(vmem_limit_bytes=2 << 20),
    )(*scalars, *own, *peer, *earlier)


def swap(array, *masks):
    peers = lax.axis_size("depth")
    pairs = [(2 * d + c, 2 * (d ^ masks[c]) + c) for d in range(peers) for c in range(2)]
    return lax.ppermute(array, AXES, pairs)


def swap_cores(array):
    return lax.ppermute(array, "samp", [(0, 1), (1, 0)])


def staged(n, act, halves, odd, weights, states, width, count):
    chans = act.shape[1]
    rows = 27 * chans
    pieces = n * n
    size = rows // (2 * pieces)
    wide = -(-size // 16) * 16
    step = 2 * size - wide
    depth = lax.axis_index("depth")
    one = lambda value: jnp.reshape(value, (1,)).astype(jnp.int32)
    core, first, second = one(lax.axis_index("samp")), one(depth % n), one(depth // n)
    f32 = lambda *shape: jax.ShapeDtypeStruct(shape, jnp.float32)
    b16 = lambda *shape: jax.ShapeDtypeStruct(shape, jnp.bfloat16)
    shift = pltpu.VMEM((1, act.shape[0] + 2 * width, 3 * chans), jnp.bfloat16)
    shifts = pltpu.VMEM((3, act.shape[0] + 2 * width, 3 * chans), jnp.bfloat16)
    flops = 2 * rows * chans * act.shape[0]
    third, chip = 9 * chans, 2 * size
    side = third // chip
    inner = pieces - 2 * side - 2
    edge = third - side * chip
    grads = pltpu.VMEM((third, chans), jnp.float32)
    filters = functools.partial(call, flops=flops // 3, limit=6 << 20)
    half = lambda count: (f32(count, wide, chans),) * 2
    edges, early, sent = filters(
        functools.partial(early_body, width, chip, step),
        (f32(2 * (chip - edge), chans), *half(inner)),
        3,
        scratch=[shift, grads],
    )(core, act, *halves[:2])
    early_come = swap_cores(sent)
    rim, near, sent = filters(
        functools.partial(near_body, width, chip, step),
        (f32(edge, chans), *half(side)),
        3,
        scratch=[shift, grads],
        scalars=2,
    )(core, odd, act, *halves[2:4])
    near_come = swap_cores(sent)
    late, sent = filters(
        functools.partial(late_body, width, chip, step),
        half(side + 2),
        5,
        scratch=[shift, grads, pltpu.VMEM((2 * chip, chans), jnp.float32)],
        scalars=2,
    )(core, odd, act, *halves[4:], edges, rim)
    late_come = swap_cores(sent)
    terms = (late, late_come, near, near_come, early, early_come)
    parts = call(
        functools.partial(merge_body, n, "first", 0, True), (f32(n, wide, chans),) * n, 6, scalars=3, scratch=[pltpu.VMEM((pieces, wide, chans), jnp.float32)]
    )(core, first, second, *terms)
    got = exchange("first", n, parts, (1, n))
    grad_input, token = call(
        functools.partial(input_body, width),
        (b16(*act.shape), f32(8, chans)),
        7,
        flops=flops,
        moved=4 << 20,
        scratch=[shifts],
        limit=6 << 20,
    )(odd, weights, *halves)
    parts = call(
        functools.partial(merge_body, n, "second", 1, False),
        (f32(1, wide, chans),) * n,
        n + 1,
        scalars=3,
    )(core, first, second, *got, token)
    got = exchange("second", n, parts, (n, 1))
    states = [s.reshape(size, chans) for s in states]
    share = call(functools.partial(share_body, count), b16(1, wide, chans), n + 3)(
        core, *got, *states
    )
    *fresh, token = call(
        functools.partial(adam_body, count),
        (f32(size, chans),) * 4 + (f32(8, chans),),
        n + 4,
    )(core, *got, *states, share)
    got = exchange("line", n, [share] * n, (n, n))
    line = call(gather_body, b16(n, wide, chans), n + 1)(core, *got, token)
    own = exchange("plane", n, [line] * n, (1, 1))
    peer = []
    for block in own:
        peer.append(swap_cores(block))
    new_weights, where = [], [list(zip(*masks_of("plane", n)))[c] for c in range(2)]
    assert where[0] == where[1]
    at = (core, first, second)
    for chosen in ((0, n - 1), tuple(range(1, n - 1))):
        groups = tuple(where[0][t] for t in chosen)
        mine, theirs = [own[t] for t in chosen], [peer[t] for t in chosen]
        new_weights = [place(n, size, rows, groups, at, mine, theirs, new_weights)]
    new_weights = new_weights[0]
    return grad_input, [x.reshape(-1) for x in fresh], new_weights


def plain(act, halves, odd, weights, states, width, count):
    chans = act.shape[1]
    rows = 27 * chans
    shift = pltpu.VMEM((3, act.shape[0] + 2 * width, 3 * chans), jnp.bfloat16)
    grads = call(
        functools.partial(all_filter_body, width),
        jax.ShapeDtypeStruct((rows, chans), jnp.float32),
        7,
        scratch=[shift],
        limit=6 << 20,
    )(odd, act, *halves)
    grad_input, _ = call(
        functools.partial(input_body, width),
        (
            jax.ShapeDtypeStruct(act.shape, jnp.bfloat16),
            jax.ShapeDtypeStruct((8, chans), jnp.float32),
        ),
        7,
        scratch=[shift],
        limit=6 << 20,
    )(odd, weights, *halves)
    total = lax.psum_scatter(grads.reshape(-1), AXES, scatter_dimension=0, tiled=True)
    master, moment, second = states
    grad = total * jnp.float32(1.0 / count**0.5)
    new_moment = 0.9 * moment + 0.1 * grad
    new_second = 0.999 * second + 0.001 * grad * grad
    new_master = master - 0.01 * (new_moment / first_fix) / (
        jnp.sqrt(new_second / second_fix) + 1e-08
    )
    whole = lax.all_gather(new_master.astype(jnp.bfloat16), AXES, axis=0, tiled=True)
    return grad_input, [grad, new_moment, new_second, new_master], whole


def neighbours(top, bottom):
    peers = lax.axis_size("depth")
    move = lambda array, pairs: lax.ppermute(array, "depth", pairs)
    partner = [(i, i ^ 1) for i in range(peers)]
    direct = [(i - 1, i) for i in range(2, peers, 2)] + [(i + 1, i) for i in range(1, peers - 1, 2)]
    relayed = [(i - 2, i) for i in range(2, peers, 2)] + [(i + 2, i) for i in range(1, peers - 1, 2)]
    partner_top = move(top, partner)
    partner_bottom = move(bottom, partner)
    other_bottom = move(bottom, direct)
    other_top = move(partner_top, relayed)
    return (top, bottom, partner_top, partner_bottom, other_top, other_bottom)


def local(n, activations, preact, out_grad, weights, master, moment, second):
    samples, planes, height, width, chans = activations.shape
    count = samples * lax.axis_size("samp") * planes * lax.axis_size("depth") * height * width
    act = activations.reshape(-1, chans)
    half = act.shape[0] // 2

    def cotangent(part):
        slope = jnp.where(preact.reshape(-1, chans)[part] > 0, jnp.float32(1.0), jnp.float32(0.01))
        return (out_grad.reshape(-1, chans)[part].astype(jnp.float32) * slope).astype(jnp.bfloat16)

    halves = neighbours(cotangent(slice(0, half)), cotangent(slice(half, None)))
    odd = jnp.reshape(lax.axis_index("depth") % 2, (1,)).astype(jnp.int32)
    taps = weights.reshape(27, chans, chans)
    states = (master, moment, second)
    if n:
        result = staged(n, act, halves, odd, taps, states, width, count)
    else:
        result = plain(act, halves, odd, taps, states, width, count)
    grad_input, fresh, whole = result
    return (grad_input.reshape(activations.shape), *fresh, whole.reshape(weights.shape))


def stages(mesh):
    n = math.isqrt(mesh.shape["depth"])
    ready = mesh.shape["samp"] == 2 and n * n == mesh.shape["depth"] and n & (n - 1) == 0
    return n if ready else 0


def solution(mesh):
    split = P("samp", "depth", None, None, None)
    shard = P(AXES)
    n = stages(mesh)

    def body(*args):
        return local(n, *args)

    return jax.shard_map(
        body,
        mesh=mesh,
        in_specs=(split, split, split, P(), shard, shard, shard),
        out_specs=(split, shard, shard, shard, shard, P()),
        check_vma=False,
    )
```
